256 devices in a mesh: tm: 32 (over z_hi, x, core), chan: 4 (over y), win: 2 (over z_lo).
Axes of the slice: x: 4, y: 4, z: 8 (z_hi: 4, z_lo: 2; z = z_hi * 2 + z_lo), core: 2. Of those that a mesh axis runs over, the one named last changes fastest.
Arguments:
- inputs: bfloat16 [131072, 512], P(('win', 'tm', 'chan')), parts along dimension 0, may hold values from -24 to 24
- cotangent: float32 [131072, 512], P(('win', 'tm', 'chan')), parts along dimension 0, may hold values from -6 to 6
- w_filter: bfloat16 [3, 2, 512, 512], replicated, may hold values from -0.1875 to 0.1875
- w_gate: bfloat16 [3, 2, 512, 512], replicated, may hold values from -0.1875 to 0.1875
- w_res: bfloat16 [3, 512, 512], replicated, may hold values from -0.25 to 0.25
Outputs:
- output: bfloat16 [131072, 512], P(('win', 'tm', 'chan')), parts along dimension 0
- input_grad: float32 [131072, 512], P(('win', 'tm', 'chan')), parts along dimension 0
- filter_grad: float32 [6, 2, 512, 512], P('win', None, 'tm', 'chan'), parts along dimension 0
- gate_grad: float32 [6, 2, 512, 512], P('win', None, 'tm', 'chan'), parts along dimension 0
- res_grad: float32 [6, 512, 512], P('win', 'tm', 'chan'), parts along dimension 0
The draws below stay inside these ranges and needn't reach their ends.
There are 2 independent parts, one for each index of `win`. The reference program is written for one: setup_inputs(seed, part) draws one part's arguments, and reference() takes and returns one part's arrays. A program takes and returns all parts, laid end to end along the dimension named above; an argument that names none is the same for every part. Nothing has to cross between parts.
All inputs are finite; a program needn't handle non-finite values.
Results may differ from the reference program's by a relative error of at most 0.018.
Values may be sent and summed in bfloat16 or wider, within the bound.
A program may use at most 128 MiB of HBM per device.

```python
import jax
import jax.numpy as jnp

C = 512
H = 512
T_DEV = 512
LAYERS = 3
TIME = 65536


def raised(entries, key, source, target, blocks, factor):
    def block_of(position):
        return (jnp.arange(entries.shape[position]) // (entries.shape[position] // blocks)).reshape((-1,) + (1,) * (entries.ndim - 1 - position))

    one_side = jax.random.permutation(key, blocks)[block_of(target)]
    far = (block_of(target) + blocks // 2) % blocks
    return jnp.where((block_of(source) == one_side) | (block_of(source) == far), factor * entries, entries)


def block_levels(rng, shape, pieces, low, top_value):
    gain, own = 1.0, jax.random.fold_in(rng, 6)
    for dim, blocks in pieces:
        draws = jnp.exp(jax.random.uniform(jax.random.fold_in(own, dim), (blocks,), jnp.float32, low / len(pieces), top_value / len(pieces)))
        gain = gain * jnp.repeat(draws, shape[dim] // blocks).reshape([-1 if axis == dim else 1 for axis in range(len(shape))])
    return gain


def normal_values(rng, shape, scale, reach, pieces=(), kind=jnp.bfloat16):
    result = scale * jax.random.normal(rng, shape, jnp.float32)
    if pieces:
        result = result * block_levels(rng, shape, pieces, -0.22, 0.18)
    return jnp.clip(result, -reach, reach).astype(kind)


def bell_draw_with(own_key, dims, deviation, limit, shards, heavy, kind=jnp.bfloat16):
    entries = deviation * jax.random.normal(own_key, dims, jnp.float32)
    if shards:
        entries = entries * block_levels(own_key, dims, shards, -0.22, 0.18)
    return jnp.clip(raised(entries, jax.random.fold_in(own_key, 3), *heavy), -limit, limit).astype(kind)


def setup_inputs(seed: int = 0, part: int = 0) -> dict:
    seeds = jax.random.split(jax.random.key(seed), 6)
    part_splits = jax.random.split(jax.random.fold_in(seeds[5], part), 6)
    return {
        "inputs": bell_draw_with(part_splits[0], (TIME, C), 1.0, 24.0, ((0, 128),), (0, 1, 128, 5.5)),
        "cotangent": normal_values(part_splits[1], (TIME, C), 1.0, 6.0, ((0, 128),), jnp.float32),
        "w_filter": normal_values(seeds[2], (LAYERS, 2, C, H), (2 * C) ** -0.5, 0.1875),
        "w_gate": normal_values(seeds[3], (LAYERS, 2, C, H), (2 * C) ** -0.5, 0.1875),
        "w_res": normal_values(seeds[4], (LAYERS, H, C), H ** -0.5, 0.25),
    }


def delay(values, steps):
    zeros = jnp.zeros((steps, values.shape[1]), values.dtype)
    return jnp.concatenate([zeros, values[:-steps]], 0)


def advance(values, steps):
    zeros = jnp.zeros((steps, values.shape[1]), values.dtype)
    return jnp.concatenate([values[steps:], zeros], 0)


def mult(left, right):
    return jnp.dot(left, right, preferred_element_type=jnp.float32)


def reference(inputs, cotangent, w_filter, w_gate, w_res):
    stream = inputs
    saved = []
    for level in range(LAYERS):
        dilation = T_DEV * 2 ** level
        delayed = delay(stream, dilation)
        filt = mult(delayed, w_filter[level, 0]) + mult(stream, w_filter[level, 1])
        gated = mult(delayed, w_gate[level, 0]) + mult(stream, w_gate[level, 1])
        tanh_f = jnp.tanh(filt)
        sig_g = jax.nn.sigmoid(gated)
        hidden = (tanh_f * sig_g).astype(jnp.bfloat16)
        saved.append((stream, delayed, tanh_f, sig_g, hidden))
        stream = (stream.astype(jnp.float32) + mult(hidden, w_res[level])).astype(jnp.bfloat16)
    adjoint = cotangent
    filter_list = [None] * LAYERS
    gate_list = [None] * LAYERS
    res_list = [None] * LAYERS
    for level in reversed(range(LAYERS)):
        dilation = T_DEV * 2 ** level
        current, delayed, tanh_f, sig_g, hidden = saved[level]
        adj_b = adjoint.astype(jnp.bfloat16)
        res_list[level] = mult(hidden.T, adj_b)
        d_hid = mult(adj_b, w_res[level].T)
        d_f = (d_hid * sig_g * (1.0 - tanh_f * tanh_f)).astype(jnp.bfloat16)
        d_g = (d_hid * tanh_f * sig_g * (1.0 - sig_g)).astype(jnp.bfloat16)
        filter_list[level] = jnp.stack([mult(delayed.T, d_f), mult(current.T, d_f)])
        gate_list[level] = jnp.stack([mult(delayed.T, d_g), mult(current.T, d_g)])
        now = mult(d_f, w_filter[level, 1].T) + mult(d_g, w_gate[level, 1].T)
        back = mult(d_f, w_filter[level, 0].T) + mult(d_g, w_gate[level, 0].T)
        adjoint = adjoint + now + advance(back, dilation)
    return (stream, adjoint, jnp.stack(filter_list), jnp.stack(gate_list), jnp.stack(res_list))
```

```python
import jax
import jax.numpy as jnp
from jax import lax
from jax.experimental import pallas as pl
from jax.experimental.pallas import tpu as pltpu
from jax.sharding import PartitionSpec as P

MESH = pl.DeviceIdType.MESH
MATS = 5
ROWS = 16
DEEP = MATS * ROWS
CUT = 48
RINGS = 5
F32 = jnp.float32
BF16 = jnp.bfloat16


def whereabouts():
    tm = lax.axis_index("tm")
    return tm // 8, (tm // 2) % 4, tm % 2, lax.axis_index("chan")


def device_at(z, x, core, y):
    return {"tm": z * 8 + x * 2 + core, "chan": y}


class Ring:
    def __init__(self, place, up, down, piece, slots, merged, sends, recvs):
        self.p, self.up, self.down = place, up, down
        self.piece, self.slots, self.merged = piece, slots, merged
        self.sends, self.recvs = sends, recvs
        self.next, self.last, self.far = (place + 1) % 4, (place + 3) % 4, (place + 2) % 4

    def copy(self, k, source, to):
        return pltpu.make_async_remote_copy(
            src_ref=source,
            dst_ref=self.slots[k],
            send_sem=self.sends.at[k],
            recv_sem=self.recvs.at[k],
            device_id=to,
            device_id_type=MESH,
        )

    def copies(self):
        return [
            self.copy(0, self.piece(self.far, 1), self.up),
            self.copy(1, self.piece(self.far, 0), self.down),
            self.copy(2, self.piece(self.next, 0), self.up),
            self.copy(3, self.piece(self.last, 1), self.down),
            self.copy(4, self.merged[0], self.up),
            self.copy(5, self.merged[1], self.down),
        ]

    def first(self):
        for c in self.copies()[:4]:
            c.start()

    def second(self):
        every = self.copies()
        every[0].wait_recv()
        self.merged[0][...] = add(self.slots[0][...], self.piece(self.next, 1)[...])
        every[4].start()
        every[1].wait_recv()
        self.merged[1][...] = add(self.slots[1][...], self.piece(self.last, 0)[...])
        every[5].start()

    def finish(self, store):
        every = self.copies()
        every[2].wait_recv()
        every[5].wait_recv()
        store(0, total(self.piece(self.p, 0)[...], self.slots[2][...], self.slots[5][...]))
        every[3].wait_recv()
        every[4].wait_recv()
        store(1, total(self.piece(self.p, 1)[...], self.slots[3][...], self.slots[4][...]))

    def drain(self):
        for c in self.copies():
            c.wait_send()


def add(a, b):
    return (a.astype(F32) + b.astype(F32)).astype(BF16)


def total(a, b, c):
    return a.astype(F32) + b.astype(F32) + c.astype(F32)


def ring_scratch(layers):
    wide, narrow = (2, 4, DEEP, 128), (2, DEEP, 128)
    return [
        pltpu.VMEM((layers, 4, 4, 4, DEEP, 128), BF16),
        pltpu.VMEM((layers, 4, 4, 4, DEEP, 128), BF16),
        pltpu.VMEM((layers, 2, 6, 4, DEEP, 128), BF16),
        pltpu.VMEM((layers, 2) + wide, BF16),
        pltpu.VMEM((layers, 2) + wide, BF16),
        pltpu.VMEM((layers, 2, 6, DEEP, 128), BF16),
        pltpu.VMEM((layers, 2) + narrow, BF16),
        pltpu.VMEM((layers, 4, DEEP, 128), BF16),
        pltpu.VMEM((layers, 6, CUT, 128), BF16),
        pltpu.VMEM((layers, 2, CUT, 128), BF16),
        pltpu.SemaphoreType.DMA((layers, RINGS, 6)),
        pltpu.SemaphoreType.DMA((layers, RINGS, 6)),
        pltpu.SemaphoreType.DMA((layers,)),
        pltpu.SemaphoreType.DMA((layers,)),
    ]


class Reduce:
    steps = 8

    def __init__(self, layer, grads, out, scratch):
        (other, sums, slots1, merged1, result1, slots2, merged2, result2, slots3, merged3, ring_send, ring_recv, core_send,
         core_recv) = scratch
        z, x, core, y = whereabouts()
        self.layer, self.core, self.grads, self.out = layer, core, grads, out
        self.other, self.sums, self.result1, self.result2 = other.at[layer], sums.at[layer], result1.at[layer], result2.at[layer]
        self.swap = pltpu.make_async_remote_copy(
            src_ref=grads.at[:, :, :, 1 - core],
            dst_ref=self.other,
            send_sem=core_send.at[layer],
            recv_sem=core_recv.at[layer],
            device_id=device_at(z, x, 1 - core, y),
            device_id_type=MESH,
        )
        along_x = (x, device_at(z, (x + 1) % 4, core, y), device_at(z, (x + 3) % 4, core, y))
        along_y = (y, device_at(z, x, core, (y + 1) % 4), device_at(z, x, core, (y + 3) % 4))
        along_z = (z, device_at((z + 1) % 4, x, core, y), device_at((z + 3) % 4, x, core, y))
        sems = lambda k: (ring_send.at[layer, k], ring_recv.at[layer, k])
        many = lambda ref, lead, n: [ref.at[lead + (i,)] for i in range(n)]
        s, r1, r2 = self.sums, self.result1, self.result2
        self.rings1 = [
            Ring(*along_x, lambda q, h: s.at[:, h, q], many(slots1, (layer, 0), 6), many(merged1, (layer, 0), 2), *sems(0)),
            Ring(*along_y, lambda q, h: s.at[q, 2 + h], many(slots1, (layer, 1), 6), many(merged1, (layer, 1), 2), *sems(1)),
        ]
        self.rings2 = [
            Ring(*along_y, lambda q, h: r1.at[0, h, q], many(slots2, (layer, 0), 6), many(merged2, (layer, 0), 2), *sems(2)),
            Ring(*along_x, lambda q, h: r1.at[1, h, q], many(slots2, (layer, 1), 6), many(merged2, (layer, 1), 2), *sems(3)),
        ]
        sizes = (CUT, DEEP - CUT)
        rows = lambda h: pl.ds(h * CUT, sizes[h])
        halves = (1, 0, 0, 1, 1, 0)
        self.rows = rows
        self.ring3 = Ring(
            *along_z,
            lambda q, h: r2.at[q, rows(h)],
            [slots3.at[layer, k, pl.ds(0, sizes[halves[k]])] for k in range(6)],
            [merged3.at[layer, k, pl.ds(0, sizes[1 - k])] for k in range(2)],
            *sems(4),
        )

    def step(self, k):
        if k == 0:
            self.swap.start()
        elif k == 1:
            self.swap.wait_recv()

            @pl.loop(0, 16)
            def _(i):
                a, b = i // 4, i % 4
                self.sums[a, b] = add(self.grads[a, b, :, self.core], self.other[a, b])

            for r in self.rings1:
                r.first()
        elif k == 2:
            for r in self.rings1:
                r.second()
        elif k == 3:
            for u, r in enumerate(self.rings1):

                def store(h, v, u=u):
                    self.result1[u, h] = v.astype(BF16)

                r.finish(store)
                self.rings2[u].first()
        elif k == 4:
            for r in self.rings2:
                r.second()
        elif k == 5:
            for u, r in enumerate(self.rings2):

                def store(h, v, u=u):
                    self.result2[2 * u + h] = v.astype(BF16)

                r.finish(store)
            self.ring3.first()
        elif k == 6:
            self.ring3.second()
        elif k == 7:

            def store(h, v):
                self.out[self.layer, self.rows(h)] = v

            self.ring3.finish(store)

    def drain(self):
        self.swap.wait_send()
        for r in [*self.rings1, *self.rings2, self.ring3]:
            r.drain()


def greet():
    z, x, core, y = whereabouts()
    barrier = pltpu.get_barrier_semaphore()
    friends = [device_at(z, x, 1 - core, y)]
    for by in (1, 3):
        friends += [
            device_at(z, (x + by) % 4, core, y),
            device_at(z, x, core, (y + by) % 4),
            device_at((z + by) % 4, x, core, y),
        ]
    for f in friends:
        pl.semaphore_signal(barrier, inc=1, device_id=f, device_id_type=MESH)
    pl.semaphore_wait(barrier, len(friends))


def reduce_kernel(grads_ref, out_ref, *scratch):
    layers = grads_ref.shape[0]
    greet()
    work = [Reduce(n, grads_ref.at[n], out_ref, scratch) for n in range(layers)]
    for w in work:
        w.step(0)
    for t in range(1, Reduce.steps + layers - 1):
        for n, w in enumerate(work):
            if 1 <= t - n < Reduce.steps:
                w.step(t - n)
    for w in work:
        w.drain()


def reduced(grads):
    layers = grads.shape[0]
    return pl.pallas_call(
        reduce_kernel,
        out_shape=jax.ShapeDtypeStruct((layers, DEEP, 128), F32),
        in_specs=[pl.BlockSpec(memory_space=pltpu.VMEM)],
        out_specs=pl.BlockSpec(memory_space=pltpu.VMEM),
        scratch_shapes=ring_scratch(layers),
        compiler_params=pltpu.CompilerParams(collective_id=0, has_side_effects=True, vmem_limit_bytes=48 << 20),
        name="reduce",
    )(grads)


def passed_along(x, axis, by):
    count = lax.axis_size(axis)
    pairs = [(i, i + by) for i in range(count) if 0 <= i + by < count]
    return lax.ppermute(x, axis, pairs)


def body(inputs, cotangent, w_filter, w_gate, w_res):
    layers, _, width, hidden_width = w_filter.shape
    stream = inputs
    saved = []
    for level in range(layers):
        hop = 2**level
        delayed = passed_along(stream, ("tm", "chan"), hop)
        paired = jnp.concatenate([delayed, stream], 1)
        filt = jnp.dot(paired, w_filter[level].reshape(2 * width, hidden_width), preferred_element_type=F32)
        gated = jnp.dot(paired, w_gate[level].reshape(2 * width, hidden_width), preferred_element_type=F32)
        tanh_f = jnp.tanh(filt)
        sig_g = jax.nn.sigmoid(gated)
        hidden = (tanh_f * sig_g).astype(BF16)
        saved.append((paired, tanh_f, sig_g, hidden))
        stream = (stream.astype(F32) + jnp.dot(hidden, w_res[level], preferred_element_type=F32)).astype(BF16)
    adjoint = cotangent
    grads = [None] * layers
    for level in reversed(range(layers)):
        hop = 2**level
        paired, tanh_f, sig_g, hidden = saved[level]
        adj_b = adjoint.astype(BF16)
        grad_r = jnp.einsum("th,tc->hc", hidden, adj_b, preferred_element_type=F32)
        d_hid = jnp.einsum("tc,hc->th", adj_b, w_res[level], preferred_element_type=F32)
        d_f = (d_hid * sig_g * (1.0 - tanh_f * tanh_f)).astype(BF16)
        d_g = (d_hid * tanh_f * sig_g * (1.0 - sig_g)).astype(BF16)
        grad_f = jnp.einsum("tc,th->ch", paired, d_f, preferred_element_type=F32)
        grad_g = jnp.einsum("tc,th->ch", paired, d_g, preferred_element_type=F32)
        both = jnp.einsum(
            "th,ch->tc", d_f, w_filter[level].reshape(2 * width, hidden_width), preferred_element_type=F32
        ) + jnp.einsum("th,ch->tc", d_g, w_gate[level].reshape(2 * width, hidden_width), preferred_element_type=F32)
        back = both[:, :width]
        now = both[:, width:]
        adjoint = adjoint + now + passed_along(back.astype(BF16), ("tm", "chan"), -hop).astype(F32)
        mats = jnp.concatenate([g.astype(BF16) for g in (grad_f, grad_g, grad_r)], 0)
        mats = mats.reshape(MATS, 32, ROWS, 4, 128).transpose(3, 1, 0, 2, 4)
        grads[level] = mats.reshape(4, 4, 4, 2, DEEP, 128)
    sums = reduced(jnp.stack(grads)).reshape(layers, MATS, ROWS, 128)
    return (stream, adjoint, sums[:, 0:2], sums[:, 2:4], sums[:, 4])


def solution(mesh):
    placed = (P(("win", "tm", "chan"), None), P(("win", "tm", "chan"), None), P(), P(), P())
    return jax.shard_map(
        body,
        mesh=mesh,
        in_specs=placed,
        out_specs=(
            P(("win", "tm", "chan"), None),
            P(("win", "tm", "chan"), None),
            P("win", None, "tm", "chan"),
            P("win", None, "tm", "chan"),
            P("win", "tm", "chan"),
        ),
        check_vma=False,
    )
```

```python
import jax
import jax.numpy as jnp
from jax import lax
from jax.experimental import pallas as pl
from jax.experimental.pallas import tpu as pltpu
from jax.sharding import PartitionSpec as P

MESH = pl.DeviceIdType.MESH
F32 = jnp.float32
BF16 = jnp.bfloat16
LAYERS = 3
C = 512
PART = 128
STREAMS = 2
R = PART // STREAMS
ROWS = 4 * R
MATS = 5
DEEP = MATS * 16
NT = 256


def whereabouts():
    tm = lax.axis_index("tm")
    return tm // 8, (tm // 2) % 4, tm % 2, lax.axis_index("chan")


def device_at(z, x, core, y):
    return {"tm": z * 8 + x * 2 + core, "chan": y}


def send(source, target, send_sem, recv_sem, to):
    return pltpu.make_async_remote_copy(
        src_ref=source, dst_ref=target, send_sem=send_sem, recv_sem=recv_sem, device_id=to, device_id_type=MESH
    )


def greet():
    z, x, core, y = whereabouts()
    tm = lax.axis_index("tm")
    barrier = pltpu.get_barrier_semaphore()
    friends = [device_at(z, x, 1 - core, y), {"tm": (tm + 1) % 32, "chan": y}, {"tm": (tm + 31) % 32, "chan": y}]
    for by in (1, 2, 3):
        friends += [
            device_at(z, (x + by) % 4, core, y),
            device_at(z, x, core, (y + by) % 4),
            device_at((z + by) % 4, x, core, y),
        ]
    for f in friends:
        pl.semaphore_signal(barrier, inc=1, device_id=f, device_id_type=MESH)
    pl.semaphore_wait(barrier, len(friends))


def dot(a, b):
    return jnp.dot(a, b, preferred_element_type=F32)


def dot_nt(a, b):
    return lax.dot_general(a, b, (((1,), (1,)), ((), ())), preferred_element_type=F32)


def total(first, *more):
    first = first.astype(F32)
    for m in more:
        first = first + m.astype(F32)
    return first


class Reduce:
    def __init__(self, layer, grads, out, s):
        z, x, core, y = whereabouts()
        self.layer, self.core, self.x, self.y, self.z = layer, core, x, y, z
        self.grads, self.out = grads.at[layer], out
        self.other, self.sums = s["other"].at[layer], s["sums"].at[layer]
        self.half, self.last = s["half"].at[layer], s["last"].at[layer]
        self.slots_x, self.slots_y = s["slots_x"].at[layer], s["slots_y"].at[layer]
        self.slots2, self.slots3 = s["slots2"].at[layer], s["slots3"].at[layer]
        self.swap = send(
            self.grads.at[:, :, :, 1 - core], self.other, s["swap_send"].at[layer], s["swap_recv"].at[layer],
            device_at(z, x, 1 - core, y),
        )
        sems = lambda k, i: (s["ring_send"].at[layer, k, i], s["ring_recv"].at[layer, k, i])
        self.copies = [[], [], [], [], []]
        for i in range(3):
            qx, qy, qz = (x + i + 1) % 4, (y + i + 1) % 4, (z + i + 1) % 4
            to_x, to_y, to_z = device_at(z, qx, core, y), device_at(z, x, core, qy), device_at(qz, x, core, y)
            for k, source, slot, to in (
                (0, self.sums.at[:, 0:2, qx], self.slots_x.at[i], to_x),
                (1, self.sums.at[qy, 2:4], self.slots_y.at[i], to_y),
                (2, self.half.at[0, qy], self.slots2.at[0, i], to_y),
                (3, self.half.at[1, qx], self.slots2.at[1, i], to_x),
                (4, self.last.at[qz], self.slots3.at[i], to_z),
            ):
                self.copies[k].append(send(source, slot, *sems(k, i), to))

    def start(self, k):
        for c in self.copies[k]:
            c.start()

    def arrived(self, k):
        for c in self.copies[k]:
            c.wait_recv()

    def step(self, k):
        if k == 0:
            self.swap.start()
        elif k == 1:
            self.swap.wait_recv()

            @pl.loop(0, 4)
            def _(a):
                self.sums[a, 0:2] = total(self.grads[a, 0:2, :, self.core], self.other[a, 0:2]).astype(BF16)

            self.start(0)

            @pl.loop(0, 4)
            def _(a):
                self.sums[a, 2:4] = total(self.grads[a, 2:4, :, self.core], self.other[a, 2:4]).astype(BF16)

            self.start(1)
        elif k == 2:
            self.arrived(0)

            @pl.loop(0, 4)
            def _(a):
                self.half[0, a] = total(self.sums[a, 0:2, self.x], *[self.slots_x[i, a] for i in range(3)]).astype(BF16)

            self.start(2)
            self.arrived(1)

            @pl.loop(0, 4)
            def _(a):
                self.half[1, a] = total(self.sums[self.y, 2:4, a], *[self.slots_y[i, :, a] for i in range(3)]).astype(BF16)

            self.start(3)
        elif k == 3:
            self.arrived(2)
            self.last[0:2] = total(self.half[0, self.y], *[self.slots2[0, i] for i in range(3)]).astype(BF16)
            self.arrived(3)
            self.last[2:4] = total(self.half[1, self.x], *[self.slots2[1, i] for i in range(3)]).astype(BF16)
            self.start(4)
        elif k == 4:
            self.arrived(4)
            self.out[self.layer] = total(self.last[self.z], *[self.slots3[i] for i in range(3)])

    def drain(self):
        self.swap.wait_send()
        for k in range(5):
            for c in self.copies[k]:
                c.wait_send()


SCRATCH = dict(
    acts=pltpu.VMEM((LAYERS, STREAMS, 8, R, C), BF16),
    final=pltpu.VMEM((STREAMS, 4, R, C), BF16),
    pre_f=pltpu.VMEM((STREAMS, ROWS, C), F32),
    pre_g=pltpu.VMEM((STREAMS, ROWS, C), F32),
    coef_f=pltpu.VMEM((LAYERS, STREAMS, ROWS, C), F32),
    coef_g=pltpu.VMEM((LAYERS, STREAMS, ROWS, C), F32),
    hidden=pltpu.VMEM((LAYERS, STREAMS, ROWS, C), BF16),
    cot=pltpu.VMEM((C, C), F32),
    cot_b=pltpu.VMEM((C, C), BF16),
    top=pltpu.VMEM((STREAMS, 4, R, C), BF16),
    adj=pltpu.VMEM((STREAMS, ROWS, C), BF16),
    gain=pltpu.VMEM((STREAMS, ROWS, C), F32),
    gain_b=pltpu.VMEM((STREAMS, 4, R, C), BF16),
    dfg=pltpu.VMEM((2, STREAMS, ROWS, C), BF16),
    back=pltpu.VMEM((LAYERS, STREAMS, 8, R, C), BF16),
    flip=pltpu.VMEM((3, C, 4 * PART), BF16),
    wf=pltpu.VMEM((LAYERS, 2, C, C), BF16),
    wg=pltpu.VMEM((LAYERS, 2, C, C), BF16),
    wr=pltpu.VMEM((LAYERS, C, C), BF16),
    grads=pltpu.VMEM((LAYERS, 4, 4, 4, 2, DEEP, 128), BF16),
    other=pltpu.VMEM((LAYERS, 4, 4, 4, DEEP, 128), BF16),
    sums=pltpu.VMEM((LAYERS, 4, 4, 4, DEEP, 128), BF16),
    slots_x=pltpu.VMEM((LAYERS, 3, 4, 2, DEEP, 128), BF16),
    slots_y=pltpu.VMEM((LAYERS, 3, 2, 4, DEEP, 128), BF16),
    half=pltpu.VMEM((LAYERS, 2, 4, 2, DEEP, 128), BF16),
    slots2=pltpu.VMEM((LAYERS, 2, 3, 2, DEEP, 128), BF16),
    last=pltpu.VMEM((LAYERS, 4, DEEP, 128), BF16),
    slots3=pltpu.VMEM((LAYERS, 3, DEEP, 128), BF16),
    ring_send=pltpu.SemaphoreType.DMA((LAYERS, 5, 3)),
    ring_recv=pltpu.SemaphoreType.DMA((LAYERS, 5, 3)),
    swap_send=pltpu.SemaphoreType.DMA((LAYERS,)),
    swap_recv=pltpu.SemaphoreType.DMA((LAYERS,)),
    load=pltpu.SemaphoreType.DMA((10,)),
    local=pltpu.SemaphoreType.DMA((4, STREAMS)),
    move_send=pltpu.SemaphoreType.DMA((4, STREAMS, 3)),
    move_recv=pltpu.SemaphoreType.DMA((4, STREAMS, 3)),
    halo_send=pltpu.SemaphoreType.DMA((2, LAYERS, STREAMS)),
    halo_recv=pltpu.SemaphoreType.DMA((2, LAYERS, STREAMS)),
)


def pass_kernel(x_ref, c_ref, wf_ref, wg_ref, wr_ref, y_ref, gain_ref, out_ref, *scratch):
    s = dict(zip(SCRATCH, scratch))
    acts, back, grads = s["acts"], s["back"], s["grads"]
    z, x, core, y = whereabouts()
    tm = lax.axis_index("tm")
    every = range(STREAMS)
    pending = []

    loads = [pltpu.make_async_copy(c_ref, s["cot"], s["load"].at[0])]
    for n in range(LAYERS):
        for k, (name, ref) in enumerate((("wf", wf_ref), ("wg", wg_ref), ("wr", wr_ref))):
            loads.append(pltpu.make_async_copy(ref.at[n], s[name].at[n], s["load"].at[1 + 3 * n + k]))
    for c in loads[1:]:
        c.start()
    loads[0].start()

    def part(ref, q, n):
        return ref.at[pl.ds(q * PART + n * R, R)]

    def moves(kind, n):
        copies = []
        for i in range(4):
            q = (y + i) % 4
            if kind == 0:
                source, target = part(x_ref, q, n), acts.at[0, n, 4 + y]
            elif kind == 1:
                source, target = part(s["cot_b"], q, n), s["top"].at[n, y]
            elif kind == 2:
                source, target = s["final"].at[n, q], part(y_ref, y, n)
            else:
                source, target = s["gain_b"].at[n, q], part(gain_ref, y, n)
            if i == 0:
                copies.append(pltpu.make_async_copy(source, target, s["local"].at[kind, n]))
            else:
                copies.append(
                    send(source, target, s["move_send"].at[kind, n, i - 1], s["move_recv"].at[kind, n, i - 1],
                         device_at(z, x, core, q))
                )
        return copies

    class Move:
        def __init__(self, kind, n):
            self.copies = moves(kind, n)

        def start(self):
            for c in self.copies[1:]:
                c.start()
            self.copies[0].start()
            pending.extend(c.wait_send for c in self.copies[1:])

        def arrived(self):
            self.copies[0].wait()
            for c in self.copies[1:]:
                c.wait_recv()

    def ahead(n, k):
        d = 2**n
        return send(acts.at[n, k, pl.ds(8 - d, d)], acts.at[n, k, pl.ds(4 - d, d)], s["halo_send"].at[0, n, k],
                    s["halo_recv"].at[0, n, k], {"tm": (tm + 1) % 32, "chan": y})

    def behind(n, k):
        d = 2**n
        return send(back.at[n, k, pl.ds(0, d)], back.at[n, k, pl.ds(4, d)], s["halo_send"].at[1, n, k],
                    s["halo_recv"].at[1, n, k], {"tm": (tm + 31) % 32, "chan": y})

    def halo_start(copy, go):
        @pl.when(go)
        def _():
            copy.start()

        def finish():
            @pl.when(go)
            def _():
                copy.wait_send()

        pending.append(finish)

    def halo_wait(copy, go):
        @pl.when(go)
        def _():
            copy.wait_recv()

    @pl.when(tm == 0)
    def _():
        for n in range(LAYERS):
            d = 2**n
            acts[n, :, 4 - d : 4] = jnp.zeros((STREAMS, d, R, C), BF16)

    @pl.when(tm == 31)
    def _():
        for n in range(LAYERS):
            d = 2**n
            back[n, :, 4 : 4 + d] = jnp.zeros((STREAMS, d, R, C), BF16)

    greet()
    enter = [Move(0, k) for k in every]
    top = [Move(1, k) for k in every]
    leave = [Move(2, k) for k in every]
    end = [Move(3, k) for k in every]
    for k in every:
        enter[k].start()

    def columns(step):
        return pl.ds(pl.multiple_of(step * NT, NT), NT)

    def tiles(count):
        return lambda f: pl.loop(0, count)(f)

    def current(n, k):
        return acts[n, k, 4:8].reshape(ROWS, C)

    def delayed(n, k):
        d = 2**n
        return acts[n, k, 4 - d : 8 - d].reshape(ROWS, C)

    def forward_now(n, k):
        @tiles(C // NT)
        def _(t):
            cols = columns(t)
            v = current(n, k)
            s["pre_f"][k, :, cols] = dot(v, s["wf"][n, 1, :, cols])
            s["pre_g"][k, :, cols] = dot(v, s["wg"][n, 1, :, cols])

    def forward_rest(n, k):
        @tiles(C // NT)
        def _(t):
            cols = columns(t)
            v = delayed(n, k)
            f = jnp.tanh(s["pre_f"][k, :, cols] + dot(v, s["wf"][n, 0, :, cols]))
            g = 0.5 + 0.5 * jnp.tanh(0.5 * (s["pre_g"][k, :, cols] + dot(v, s["wg"][n, 0, :, cols])))
            h = f * g
            s["hidden"][n, k, :, cols] = h.astype(BF16)
            s["coef_f"][n, k, :, cols] = g - f * h
            s["coef_g"][n, k, :, cols] = h - h * g

        @tiles(C // NT)
        def _(t):
            cols = columns(t)
            v = acts[n, k, 4:8, :, cols].reshape(ROWS, NT).astype(F32)
            v = (v + dot(s["hidden"][n, k], s["wr"][n, :, cols])).astype(BF16).reshape(4, R, NT)
            if n + 1 < LAYERS:
                acts[n + 1, k, 4:8, :, cols] = v
            else:
                s["final"][k, :, :, cols] = v

    for n in range(LAYERS):
        for k in every:
            if n == 0:
                enter[k].arrived()
                halo_start(ahead(0, k), tm < 31)
                if k == 0:
                    for c in loads[1:4]:
                        c.wait()
            forward_now(n, k)
        if n == 0:
            loads[0].wait()
            s["cot_b"][...] = s["cot"][...].astype(BF16)
            for k in every:
                top[k].start()
        for k in every:
            halo_wait(ahead(n, k), tm > 0)
            forward_rest(n, k)
            if n + 1 < LAYERS:
                halo_start(ahead(n + 1, k), tm < 31)
            else:
                leave[k].start()
        if n + 1 < LAYERS:
            for c in loads[4 + 3 * n : 7 + 3 * n]:
                c.wait()

    def adjoint(n, k):
        if n == LAYERS - 1:
            top[k].arrived()
            return
        d = 2 ** (n + 1)
        s["gain"][k] += back[n + 1, k, d : 4 + d].reshape(ROWS, C).astype(F32)
        s["adj"][k] = (s["gain"][k] + s["top"][k].reshape(ROWS, C).astype(F32)).astype(BF16)

    def gates(n, k):
        @tiles(C // NT)
        def _(t):
            cols = columns(t)
            v = s["top"][k].reshape(ROWS, C) if n == LAYERS - 1 else s["adj"][k]
            dh = dot_nt(v, s["wr"][n, cols, :])
            s["dfg"][0, k, :, cols] = (dh * s["coef_f"][n, k, :, cols]).astype(BF16)
            s["dfg"][1, k, :, cols] = (dh * s["coef_g"][n, k, :, cols]).astype(BF16)

    def both(n, k, tap, rows):
        return dot_nt(s["dfg"][0, k], s["wf"][n, tap, rows, :]) + dot_nt(s["dfg"][1, k], s["wg"][n, tap, rows, :])

    def backward_far(n, k):
        @tiles(C // NT)
        def _(t):
            cols = columns(t)
            back[n, k, 0:4, :, cols] = both(n, k, 0, cols).astype(BF16).reshape(4, R, NT)

    def backward_now(n, k):
        @tiles(C // NT)
        def _(t):
            cols = columns(t)
            if n == LAYERS - 1:
                s["gain"][k, :, cols] = both(n, k, 1, cols)
            else:
                s["gain"][k, :, cols] += both(n, k, 1, cols)

    def weights(n):
        for k in every:
            cols = pl.ds(k * ROWS, ROWS)
            s["flip"][0, :, cols] = delayed(n, k).T
            s["flip"][1, :, cols] = current(n, k).T
            s["flip"][2, :, cols] = s["hidden"][n, k].T

        def store(value, m, t):
            value = value.astype(BF16)
            for j in range(NT // 128):
                grads[n, (NT // 128) * t + j, :, :, :, m * 16 : m * 16 + 16, :] = value[:, j * 128 : j * 128 + 128].reshape(
                    4, 4, 2, 16, 128
                )

        @tiles(C // NT)
        def _(t):
            cols = columns(t)
            for m in range(4):
                d = s["dfg"][m // 2, :, :, cols].reshape(4 * PART, NT)
                store(dot(s["flip"][m % 2], d), m, t)
            if n == LAYERS - 1:
                d = s["top"][:, :, :, cols].reshape(4 * PART, NT)
            else:
                d = s["adj"][:, :, cols].reshape(4 * PART, NT)
            store(dot(s["flip"][2], d), 4, t)

    work = [Reduce(n, grads, out_ref, s) for n in range(LAYERS)]
    for n in reversed(range(LAYERS)):
        for k in every:
            if n + 1 < LAYERS:
                halo_wait(behind(n + 1, k), tm < 31)
            adjoint(n, k)
            gates(n, k)
            if n:
                backward_far(n, k)
                halo_start(behind(n, k), tm > 0)
        if n:
            if n + 1 < LAYERS:
                work[n + 1].step(1)
            for k in every:
                backward_now(n, k)
            if n + 1 < LAYERS:
                work[n + 1].step(2)
            weights(n)
            work[n].step(0)
            if n + 1 < LAYERS:
                work[n + 1].step(3)
        else:
            work[1].step(1)
            weights(0)
            work[0].step(0)
            for k in every:
                backward_far(0, k)
                halo_start(behind(0, k), tm > 0)
            work[0].step(1)
            work[1].step(2)
            for k in every:
                backward_now(0, k)
            for k in every:
                halo_wait(behind(0, k), tm < 31)
                s["gain_b"][k] = (s["gain"][k] + back[0, k, 1:5].reshape(ROWS, C).astype(F32)).astype(BF16).reshape(4, R, C)
                end[k].start()
            work[0].step(2)
            work[1].step(3)
            work[0].step(3)
            work[2].step(4)
            work[1].step(4)
            work[0].step(4)
    for k in every:
        leave[k].arrived()
        end[k].arrived()
    for w in work:
        w.drain()
    for p in pending:
        p()


def body(inputs, cotangent, w_filter, w_gate, w_res):
    anywhere = pl.BlockSpec(memory_space=pl.ANY)
    out, gain, sums = pl.pallas_call(
        pass_kernel,
        out_shape=(
            jax.ShapeDtypeStruct(inputs.shape, BF16),
            jax.ShapeDtypeStruct(inputs.shape, BF16),
            jax.ShapeDtypeStruct((LAYERS, DEEP, 128), F32),
        ),
        in_specs=[anywhere] * 5,
        out_specs=(anywhere, anywhere, pl.BlockSpec(memory_space=pltpu.VMEM)),
        scratch_shapes=list(SCRATCH.values()),
        compiler_params=pltpu.CompilerParams(collective_id=0, has_side_effects=True, vmem_limit_bytes=63 << 20),
        name="training_pass",
    )(inputs, cotangent, w_filter, w_gate, w_res)
    sums = sums.reshape(LAYERS, MATS, 16, 128)
    return (out, cotangent + gain.astype(F32), sums[:, 0:2], sums[:, 2:4], sums[:, 4])


def solution(mesh):
    rows = P(("win", "tm", "chan"), None)
    return jax.shard_map(
        body,
        mesh=mesh,
        in_specs=(rows, rows, P(), P(), P()),
        out_specs=(rows, rows, P("win", None, "tm", "chan"), P("win", None, "tm", "chan"), P("win", "tm", "chan")),
        check_vma=False,
    )
```
